128 devices in a mesh: req: 32 (over x, y, core), mlp: 4 (over z).
Axes of the slice: x: 4, y: 4, z: 4, core: 2. Of those that a mesh axis runs over, the one named last changes fastest.
Arguments:
- hidden_in: bfloat16 [64, 512, 2048], P('req'), may hold values from -6 to 6
- lengths: int32 [64], replicated, may hold values from 1 to 512, 16384 in all
- slot_request: int32 [64], replicated, may hold values from 0 to 63, each once
- adapter_of: int32 [64], replicated, may hold values from 0 to 63, as said below
- adapter_slot: int32 [64], replicated, may hold values from 0 to 63, each once
- norm_gain_attn: float32 [2048], replicated, may hold values from 0.5 to 1.5
- norm_gain_mlp: float32 [2048], replicated, may hold values from 0.5 to 1.5
- final_gain: float32 [2048], replicated, may hold values from 0.5 to 1.5
- w_qkv: bfloat16 [2048, 3, 2048], P(None, None, 'mlp')
- w_out: bfloat16 [2048, 2048], P('mlp'), may hold values from -0.125 to 0.125
- w_gateup: bfloat16 [2048, 2, 4096], P('req', None, 'mlp'), may hold values from -0.125 to 0.125
- w_down: bfloat16 [4096, 2048], P('mlp', 'req'), may hold values from -0.09375 to 0.09375
- adapter_down: bfloat16 [64, 16, 2048], P('req'), may hold values from -0.125 to 0.125
- adapter_up: bfloat16 [64, 16, 2048], P('req', None, 'mlp'), may hold values from -1.5 to 1.5
- vocab: bfloat16 [49152, 2048], P(('req', 'mlp')), may hold values from -0.375 to 0.375
Outputs:
- out_hidden: bfloat16 [64, 512, 2048], P('req')
- request_norm: float32 [64], replicated
- request_peak: float32 [64], replicated
The draws below stay inside these ranges and needn't reach their ends.
Inputs may be any that keep to these rules, and one draw needn't show every extreme that they name: Some request has exactly 512 tokens, and all lengths together sum to 16384. `slot_request`: each request sits in exactly one slot. `adapter_of`: exactly 16 distinct adapters are named. `adapter_slot`: each adapter sits in exactly one row of the adapter tables.
All inputs are finite; a program needn't handle non-finite values.
Results may differ from the reference program's by a relative error of at most 0.018.
Values may be sent and summed in bfloat16 or wider, within the bound.
A program may use at most 128 MiB of HBM per device.

```python
import math
import jax
import jax.numpy as jnp
import numpy as np
from jax import lax

D = 2048
ATTENTION_HEADS = 32
HEAD_WIDTH = 64
FF = 4096
VOCAB = 49152
ADAPTERS = 64
ACTIVE = 16
RANK = 16
TOKEN_SLOTS = 512
R = 64
N_MLP = 4


def draw_adapter_of(key, part):
    key_one, key_two, key_three, key_four = jax.random.split(key, 4)
    chosen = jax.random.permutation(key_one, ADAPTERS)[:ACTIVE]
    order = jax.random.permutation(key_two, R)
    first_draw = jax.random.randint(key_three, (R,), 0, ACTIVE)
    second_draw = jax.random.randint(key_four, (R,), 0, ACTIVE)
    skewed = first_draw * second_draw // ACTIVE
    choose_index = jnp.where(order < ACTIVE, order, skewed)
    return jnp.take(chosen, choose_index).astype(jnp.int32)


def draw_w_qkv(key, part):
    own_key = jax.random.fold_in(key, 7013)
    key_base, key_heads, key_strength = jax.random.split(own_key, 3)
    base = jnp.clip(jax.random.normal(key_base, (D, 3, D), jnp.float32), -6.0, 6.0) * D ** (-0.5)
    strong_count = max(1, ATTENTION_HEADS // 8)
    head_order = jax.random.permutation(key_heads, ATTENTION_HEADS)
    strong_heads = head_order < strong_count
    strength = jax.random.uniform(key_strength, (ATTENTION_HEADS,), jnp.float32, 150.0, 400.0) * HEAD_WIDTH ** (-0.5)
    strong_columns = jnp.repeat(strong_heads, HEAD_WIDTH)
    factor_columns = jnp.repeat(strength, HEAD_WIDTH)
    query_part = base[:, 0, :]
    key_part = jnp.where(strong_columns[None, :], query_part * factor_columns[None, :], base[:, 1, :])
    joined = jnp.stack([query_part, key_part, base[:, 2, :]], axis=1)
    return joined.astype(jnp.bfloat16)


def block_levels(stream_key, extent, shards, least, high):
    factor_of = 1.0
    for axis_at, parts in shards:
        steps = jax.random.uniform(jax.random.fold_in(jax.random.fold_in(stream_key, 6), axis_at), (parts,), jnp.float32, least / len(shards), high / len(shards))
        factor_of = factor_of * jnp.repeat(jnp.exp(steps), extent[axis_at] // parts).reshape((-1,) + (1,) * (len(extent) - 1 - axis_at))
    return factor_of


def split_up(number_of, total, most, slope):
    portions = [(1 << 20) // math.isqrt(standing ** slope) + 1 for standing in range(2, number_of + 1)]
    spare, given = total - most - (number_of - 1), [1] * (number_of - 1)
    while spare > 0:
        free = [i for i in range(number_of - 1) if given[i] < most]
        pool, budget = sum([portions[i] for i in free]), spare
        for i in free:
            addition = min(most - given[i], max(1, budget * portions[i] // pool), spare)
            given[i] = given[i] + addition
            spare = spare - addition
    return np.array([most] + given)


def ragged_sizes(key, amount, total, limit, skew):
    if amount == 2:
        one = jax.random.randint(key, (), max(1, total - limit), min(limit, total - 1) + 1)
        return jnp.stack([one, total - one])
    tallies = jnp.asarray(split_up(amount, total, limit, skew), jnp.int32)
    couples = (amount - 1) // 2
    giver, taker = tallies[1:1 + 2 * couples:2], tallies[2:2 + 2 * couples:2]
    margin = jnp.minimum(giver - 1, limit - taker)
    moved = jax.random.randint(jax.random.fold_in(key, 1), (couples,), 0, 1 << 20) % (margin + 1)
    tallies = tallies.at[1:1 + 2 * couples:2].set(giver - moved).at[2:2 + 2 * couples:2].set(taker + moved)
    return tallies[jax.random.permutation(jax.random.fold_in(key, 2), amount)]


def normal_values(rng, dims, scale, bound, cuts=(), kind=jnp.bfloat16):
    array = scale * jax.random.normal(rng, dims, jnp.float32)
    if cuts:
        array = array * block_levels(rng, dims, cuts, -0.22, 0.18)
    return jnp.clip(array, -bound, bound).astype(kind)


def setup_inputs(seed: int = 0) -> dict:
    key_list = jax.random.split(jax.random.key(seed), 16)
    hidden_in = normal_values(key_list[0], (R, TOKEN_SLOTS, D), 1.0, 6.0, ((0, 32),))
    lengths = ragged_sizes(key_list[1], R, R * TOKEN_SLOTS // 2, TOKEN_SLOTS, 2).astype(jnp.int32)
    slot_request = jax.random.permutation(key_list[2], R).astype(jnp.int32)
    adapter_of = draw_adapter_of(jax.random.fold_in(key_list[15], 71), 0)
    adapter_slot = jax.random.permutation(key_list[4], ADAPTERS).astype(jnp.int32)
    norm_gain_attn = jnp.clip(1.0 + 0.1 * jax.random.normal(key_list[5], (D,), jnp.float32), 0.5, 1.5)
    norm_gain_mlp = jnp.clip(1.0 + 0.1 * jax.random.normal(key_list[6], (D,), jnp.float32), 0.5, 1.5)
    final_gain = jnp.clip(1.0 + 0.1 * jax.random.normal(key_list[7], (D,), jnp.float32), 0.5, 1.5)
    w_qkv = draw_w_qkv(jax.random.fold_in(key_list[15], 71), 0)
    w_out = normal_values(key_list[9], (D, D), D ** -0.5, 0.125, ((0, 4),))
    w_gateup = normal_values(key_list[10], (D, 2, FF), D ** -0.5, 0.125, ((0, 32), (2, 4)))
    w_down = normal_values(key_list[11], (FF, D), FF ** -0.5, 0.09375, ((0, 4), (1, 32)))
    adapter_down = normal_values(key_list[12], (ADAPTERS, RANK, D), D ** -0.5, 0.125, ((0, 32),))
    adapter_up = normal_values(key_list[13], (ADAPTERS, RANK, D), RANK ** -0.5, 1.5, ((0, 32), (2, 4)))
    vocab = normal_values(key_list[14], (VOCAB, D), (D // 9) ** -0.5, 0.375, ((0, 128),))
    return dict(hidden_in=hidden_in, lengths=lengths, slot_request=slot_request, adapter_of=adapter_of, adapter_slot=adapter_slot, norm_gain_attn=norm_gain_attn, norm_gain_mlp=norm_gain_mlp, final_gain=final_gain, w_qkv=w_qkv, w_out=w_out, w_gateup=w_gateup, w_down=w_down, adapter_down=adapter_down, adapter_up=adapter_up, vocab=vocab)


EPSILON = 1e-05
ROPE_BASE = 130000.0
ADAPTER_SCALE = 2.0
MASKED = -1e+30

def rms_norm(values, gain):
    return values * lax.rsqrt(lax.optimization_barrier(jnp.mean(values * values, axis=-1, keepdims=True)) + EPSILON) * gain

def rotary_embedded(tensor):
    length = tensor.shape[-3]
    half_width = tensor.shape[-1] // 2
    frequency = ROPE_BASE ** (-(jnp.arange(half_width, dtype=jnp.float32) * 2.0 / tensor.shape[-1]))
    angles = jnp.arange(length, dtype=jnp.float32)[:, None] * frequency[None, :]
    cosine = jnp.cos(angles)[:, None, :]
    sine_part = jnp.sin(angles)[:, None, :]
    front_half = tensor[..., :half_width]
    back_half = tensor[..., half_width:]
    return jnp.concatenate([front_half * cosine - back_half * sine_part, back_half * cosine + front_half * sine_part], axis=-1)

def reference(hidden_in, lengths, slot_request, adapter_of, adapter_slot, norm_gain_attn, norm_gain_mlp, final_gain, w_qkv, w_out, w_gateup, w_down, adapter_down, adapter_up, vocab):
    slot_lengths = jnp.take(lengths, slot_request)
    slot_tables = jnp.take(adapter_slot, jnp.take(adapter_of, slot_request))
    positions = jnp.arange(TOKEN_SLOTS)
    group_heads = D // N_MLP
    group_units = FF // N_MLP

    def one_slot(slot_items):
        hidden, length, table_row = slot_items
        residual_in = hidden.astype(jnp.float32)
        normed = rms_norm(residual_in, norm_gain_attn).astype(jnp.bfloat16)
        projected_rows = jnp.dot(normed, w_qkv.reshape(D, 3 * D), preferred_element_type=jnp.float32).reshape(TOKEN_SLOTS, 3, D)
        down_one = lax.dynamic_index_in_dim(adapter_down, table_row, 0, keepdims=False)
        up_one = lax.dynamic_index_in_dim(adapter_up, table_row, 0, keepdims=False)
        low_rank = jnp.dot(normed, down_one.T, preferred_element_type=jnp.float32).astype(jnp.bfloat16)
        raised_rows = jnp.dot(low_rank, up_one, preferred_element_type=jnp.float32)
        query_head_rows = rotary_embedded((projected_rows[:, 0] + ADAPTER_SCALE * raised_rows).reshape(TOKEN_SLOTS, ATTENTION_HEADS, HEAD_WIDTH)).astype(jnp.bfloat16)
        key_heads = rotary_embedded(projected_rows[:, 1].reshape(TOKEN_SLOTS, ATTENTION_HEADS, HEAD_WIDTH)).astype(jnp.bfloat16)
        value_heads = projected_rows[:, 2].reshape(TOKEN_SLOTS, ATTENTION_HEADS, HEAD_WIDTH).astype(jnp.bfloat16)
        scores = jnp.einsum('qhd,khd->hqk', query_head_rows.astype(jnp.float32), key_heads.astype(jnp.float32)) * HEAD_WIDTH ** (-0.5)
        allowed = (positions[None, :] <= positions[:, None]) & (positions[None, :] < length)
        scores = jnp.where(allowed[None], scores, MASKED)
        probabilities = jax.nn.softmax(scores, axis=-1).astype(jnp.bfloat16)
        attended = jnp.einsum('hqk,khd->qhd', probabilities.astype(jnp.float32), value_heads.astype(jnp.float32)).astype(jnp.bfloat16).reshape(TOKEN_SLOTS, D)
        head_parts = jnp.einsum('sgc,gcd->gsd', attended.reshape(TOKEN_SLOTS, N_MLP, group_heads).astype(jnp.float32), w_out.reshape(N_MLP, group_heads, D).astype(jnp.float32)).astype(jnp.bfloat16)
        head_parts = lax.optimization_barrier(head_parts)
        mixed_heads = lax.optimization_barrier(jnp.sum(head_parts.astype(jnp.float32), axis=0))
        stream = (residual_in + mixed_heads).astype(jnp.bfloat16)
        normed_mid = rms_norm(stream.astype(jnp.float32), norm_gain_mlp).astype(jnp.bfloat16)
        gate_up = jnp.dot(normed_mid, w_gateup.reshape(D, 2 * FF), preferred_element_type=jnp.float32).reshape(TOKEN_SLOTS, 2, FF)
        activated = (jax.nn.silu(gate_up[:, 0]) * gate_up[:, 1]).astype(jnp.bfloat16)
        unit_parts = jnp.einsum('sgc,gcd->gsd', activated.reshape(TOKEN_SLOTS, N_MLP, group_units).astype(jnp.float32), w_down.reshape(N_MLP, group_units, D).astype(jnp.float32)).astype(jnp.bfloat16)
        unit_parts = lax.optimization_barrier(unit_parts)
        unit_sum = lax.optimization_barrier(jnp.sum(unit_parts.astype(jnp.float32), axis=0))
        result = stream.astype(jnp.float32) + unit_sum
        out_slot = jnp.where((positions < length)[:, None], result, 0.0).astype(jnp.bfloat16)
        out_float = out_slot.astype(jnp.float32)
        slot_norm = jnp.sqrt(jnp.sum(out_float * out_float) / (length.astype(jnp.float32) * D))
        last_row = lax.dynamic_index_in_dim(out_float, (length - 1).astype(jnp.int32), 0, keepdims=False)
        last_normed = rms_norm(last_row, final_gain).astype(jnp.bfloat16)
        slot_peak = jnp.max(jnp.dot(vocab, last_normed, preferred_element_type=jnp.float32))
        return (out_slot, slot_norm, slot_peak)
    out_hidden, slot_norm, slot_peak = lax.map(one_slot, (hidden_in, slot_lengths, slot_tables))
    request_norm = jnp.zeros((R,), jnp.float32).at[slot_request].set(slot_norm)
    request_peak = jnp.zeros((R,), jnp.float32).at[slot_request].set(slot_peak)
    return (out_hidden, request_norm, request_peak)
```

```python
import functools

import jax
import jax.numpy as jnp
import numpy as np
from jax import lax
from jax.experimental import pallas as pl
from jax.experimental.pallas import tpu as pltpu
from jax.sharding import PartitionSpec as P

HEAD_WIDTH = 64
EPSILON = 1e-05
ROPE_BASE = 130000.0
ADAPTER_SCALE = 2.0
MASKED = -1e30
MESH = pl.DeviceIdType.MESH
F32 = jnp.float32
BF16 = jnp.bfloat16
SIDE = 4


def rms_norm(values, gain):
    return values * lax.rsqrt(jnp.mean(values * values, axis=-1, keepdims=True) + EPSILON) * gain


def rope_tables(length):
    half = HEAD_WIDTH // 2
    frequency = ROPE_BASE ** (-(np.arange(half, dtype=np.float64) * 2.0 / HEAD_WIDTH))
    angles = np.arange(length, dtype=np.float64)[:, None] * frequency[None, :]
    cosine, sine = np.cos(angles), np.sin(angles)
    cosines = np.concatenate([cosine, cosine] * 2, axis=1).astype(np.float32)
    sines = np.concatenate([-sine, sine] * 2, axis=1).astype(np.float32)
    return cosines, sines


def dot(a, b):
    return jnp.dot(a, b, preferred_element_type=F32)


def dot_t(a, b):
    return lax.dot_general(a, b, (((1,), (1,)), ((), ())), preferred_element_type=F32)


def layer_kernel(
    rows_ref, gain_attn, gain_mlp, cos_ref, sin_ref,
    hid_h, wqkv_h, wout_h, wts_h, adp_h,
    out_h,
    hid, wqkv, nrm, qb, kb, vb, att, wo, wts, adp, dsel, part, act, outb, xbuf, rbuf, ybuf,
    local_sem, send_sem, recv_sem,
):
    me = lax.axis_index("req")
    z = lax.axis_index("mlp")
    x, y, c = me // 8, (me // 2) % SIDE, me % 2
    nx, px = lax.rem(x + 1, SIDE), lax.rem(x + 3, SIDE)
    ny, py = lax.rem(y + 1, SIDE), lax.rem(y + 3, SIDE)
    nz, pz, oz = lax.rem(z + 1, SIDE), lax.rem(z + 3, SIDE), lax.rem(z + 2, SIDE)
    ox, oy = lax.rem(x + 2, SIDE), lax.rem(y + 2, SIDE)

    def at(xx, yy):
        return (xx * 8 + yy * 2 + c, z)

    xp, xm, yp, ym = at(nx, y), at(px, y), at(x, ny), at(x, py)
    zp, zm, zo = (me, nz), (me, pz), (me, oz)
    twin = (x * 8 + y * 2 + (1 - c), z)

    barrier = pltpu.get_barrier_semaphore()
    for other in (xp, xm, yp, ym, zp, zm, zo, twin):
        pl.semaphore_signal(barrier, inc=1, device_id=other, device_id_type=MESH)
    pl.semaphore_wait(barrier, 8)

    sent = []

    def send(src, dst, to):
        i = len(sent)
        copy = pltpu.make_async_remote_copy(
            src_ref=src, dst_ref=dst, send_sem=send_sem.at[i], recv_sem=recv_sem.at[i],
            device_id=to, device_id_type=MESH,
        )
        copy.start()
        sent.append(copy)
        return copy

    locals_ = []

    def fetch(src, dst):
        copy = pltpu.make_async_copy(src, dst, local_sem.at[len(locals_)])
        copy.start()
        locals_.append(copy)
        return copy

    def gather_xy(src, full):
        width = src.shape[-1] // 2
        left, right = pl.ds(0, width), pl.ds(width, width)
        state = {}

        def step0():
            state["own"] = fetch(src, full.at[x, y, c])
            own_l, own_r = full.at[x, y, c, :, :, left], full.at[x, y, c, :, :, right]
            state["a"] = [
                send(src.at[:, :, left], own_l, xp), send(src.at[:, :, left], own_l, xm),
                send(src.at[:, :, right], own_r, yp), send(src.at[:, :, right], own_r, ym),
            ]

        def step1():
            for copy in state["a"]:
                copy.wait_recv()
            state["b"] = [
                send(full.at[px, y, c, 0:1, :, left], full.at[px, y, c, 0:1, :, left], xp),
                send(full.at[nx, y, c, 1:2, :, left], full.at[nx, y, c, 1:2, :, left], xm),
                send(full.at[x, py, c, 0:1, :, right], full.at[x, py, c, 0:1, :, right], yp),
                send(full.at[x, ny, c, 1:2, :, right], full.at[x, ny, c, 1:2, :, right], ym),
            ]

        def step2():
            state["own"].wait()
            for copy in state["b"]:
                copy.wait_recv()
            line_l, line_r = full.at[:, y, c, :, :, left], full.at[x, :, c, :, :, right]
            state["c"] = [
                send(line_l, line_l, yp), send(line_l, line_l, ym),
                send(line_r, line_r, xp), send(line_r, line_r, xm),
            ]
            state["t"] = [send(line_l, line_l, twin), send(line_r, line_r, twin)]

        def step3():
            for copy in state["c"]:
                copy.wait_recv()
            state["d"] = [
                send(full.at[0:2, py, c, :, :, left], full.at[0:2, py, c, :, :, left], yp),
                send(full.at[2:4, ny, c, :, :, left], full.at[2:4, ny, c, :, :, left], ym),
                send(full.at[px, 0:2, c, :, :, right], full.at[px, 0:2, c, :, :, right], xp),
                send(full.at[nx, 2:4, c, :, :, right], full.at[nx, 2:4, c, :, :, right], xm),
            ]
            for yy in (py, ny):
                state["t"].append(send(full.at[:, yy, c, :, :, left], full.at[:, yy, c, :, :, left], twin))
            for xx in (px, nx):
                state["t"].append(send(full.at[xx, :, c, :, :, right], full.at[xx, :, c, :, :, right], twin))

        def step4():
            for copy in state["d"]:
                copy.wait_recv()
            state["t"].append(send(full.at[:, oy, c, :, :, left], full.at[:, oy, c, :, :, left], twin))
            state["t"].append(send(full.at[ox, :, c, :, :, right], full.at[ox, :, c, :, :, right], twin))

        def step5():
            for copy in state["t"]:
                copy.wait_recv()

        return [step0, step1, step2, step3, step4, step5]

    adp_steps = gather_xy(adp_h, adp)
    wts_steps = gather_xy(wts_h, wts)
    wo_state = {}

    def wo_step0():
        mine = pl.ds(pl.multiple_of(c * 256, 256), 256)
        wo_state["own"] = fetch(wout_h, wo.at[z])
        wo_state["a"] = [
            send(wout_h.at[mine], wo.at[z, mine], zp), send(wout_h.at[mine], wo.at[z, mine], zm),
        ]

    def wo_step1():
        mine = pl.ds(pl.multiple_of(c * 256, 256), 256)
        low = pl.ds(pl.multiple_of(c * 256, 256), 128)
        high = pl.ds(pl.multiple_of(c * 256 + 128, 128), 128)
        for copy in wo_state["a"]:
            copy.wait_recv()
        wo_state["b"] = [
            send(wo.at[pz, low], wo.at[pz, low], zp), send(wo.at[nz, high], wo.at[nz, high], zm),
        ]
        wo_state["t"] = [
            send(wo.at[pz, mine], wo.at[pz, mine], twin), send(wo.at[nz, mine], wo.at[nz, mine], twin),
        ]

    def wo_step2():
        mine = pl.ds(pl.multiple_of(c * 256, 256), 256)
        for copy in wo_state["b"]:
            copy.wait_recv()
        wo_state["t"].append(send(wo.at[oz, mine], wo.at[oz, mine], twin))

    def wo_step3():
        wo_state["own"].wait()
        for copy in wo_state["t"]:
            copy.wait_recv()

    hid_copy = fetch(hid_h, hid)
    adp_steps[0]()
    wqkv_copy = fetch(wqkv_h, wqkv)
    wts_steps[0]()
    wo_step0()

    def normalise(slot, gain):
        def body(i, _):
            rows = pl.ds(pl.multiple_of(i * 32, 32), 32)
            values = hid[slot, rows, :].astype(F32)
            nrm[slot, rows, :] = rms_norm(values, gain[...]).astype(BF16)
            return 0

        lax.fori_loop(0, 16, body, 0)

    lane = lax.broadcasted_iota(jnp.int32, (512, 128), 1)
    first_half = lax.rem(lane, 64) < 32

    def rotate(values):
        swapped = jnp.where(first_half, pltpu.roll(values, 96, 1), pltpu.roll(values, 32, 1))
        return values * cos_ref[...] + swapped * sin_ref[...]

    def keys_values(slot):
        def body(i, _):
            cols = pl.ds(pl.multiple_of(i * 256, 256), 256)
            keys = dot(nrm[slot], wqkv[1, :, cols])
            kb[slot, :, pl.ds(pl.multiple_of(i * 256, 256), 128)] = rotate(keys[:, :128]).astype(BF16)
            kb[slot, :, pl.ds(pl.multiple_of(i * 256 + 128, 128), 128)] = rotate(keys[:, 128:]).astype(BF16)
            vb[slot, :, cols] = dot(nrm[slot], wqkv[2, :, cols]).astype(BF16)
            return 0

        lax.fori_loop(0, 2, body, 0)

    def queries(slot):
        low = dot_t(nrm[slot, :, 0:512], dsel[0, slot])
        for zz in range(1, SIDE):
            low += dot_t(nrm[slot, :, zz * 512:(zz + 1) * 512], dsel[zz, slot])
        low = low.astype(BF16)
        t = rows_ref[slot]
        r = t // 2

        def body(i, _):
            cols = pl.ds(pl.multiple_of(i * 256, 256), 256)
            up = adp[r // 8, (r // 2) % SIDE, r % 2, t % 2][16:32]
            up_low, up_high = up[:, :256], up[:, 256:]
            up_cols = jnp.where(i == 0, up_low, up_high)
            values = dot(nrm[slot], wqkv[0, :, cols]) + ADAPTER_SCALE * dot(low, up_cols)
            scale = HEAD_WIDTH ** (-0.5)
            qb[slot, :, pl.ds(pl.multiple_of(i * 256, 256), 128)] = (rotate(values[:, :128]) * scale).astype(BF16)
            qb[slot, :, pl.ds(pl.multiple_of(i * 256 + 128, 128), 128)] = (rotate(values[:, 128:]) * scale).astype(BF16)
            return 0

        lax.fori_loop(0, 2, body, 0)

    lane_q = lax.broadcasted_iota(jnp.int32, (128, 128), 1) < 64
    causal = lax.broadcasted_iota(jnp.int32, (128, 128), 1) <= lax.broadcasted_iota(jnp.int32, (128, 128), 0)
    causal2 = jnp.concatenate([causal, causal], axis=0)

    def attention(slot):
        def body(i, _):
            cols = pl.ds(pl.multiple_of(i * 128, 128), 128)
            for j in range(4):
                q = qb[slot, j * 128:(j + 1) * 128, cols]
                zero = jnp.zeros_like(q)
                both = jnp.concatenate([jnp.where(lane_q, q, zero), jnp.where(lane_q, zero, q)], axis=0)
                n = (j + 1) * 128
                scores = dot_t(both, kb[slot, 0:n, cols])
                diag = jnp.where(causal2, scores[:, n - 128:], MASKED)
                scores = diag if j == 0 else jnp.concatenate([scores[:, :n - 128], diag], axis=1)
                top = jnp.max(scores, axis=1, keepdims=True)
                weights = jnp.exp(scores - top)
                total = jnp.sum(weights, axis=1, keepdims=True)
                mixed = dot(weights.astype(BF16), vb[slot, 0:n, cols]) / total
                att[slot, z, j * 128:(j + 1) * 128, cols] = jnp.where(lane_q, mixed[:128], mixed[128:]).astype(BF16)
            return 0

        lax.fori_loop(0, 4, body, 0)

    att_state = {}

    def att_send(slot):
        mine = att.at[slot, z]
        att_state[slot] = [send(mine, mine, zp), send(mine, mine, zm)]

    def att_forward(slot):
        for copy in att_state[slot]:
            copy.wait_recv()
        low, high = att.at[slot, pz, 0:256], att.at[slot, nz, 256:512]
        att_state[slot] = [send(low, low, zp), send(high, high, zm)]

    def att_done(slot):
        for copy in att_state[slot]:
            copy.wait_recv()

    hid_copy.wait()
    normalise(0, gain_attn)
    adp_steps[1]()
    normalise(1, gain_attn)
    adp_steps[2]()
    wqkv_copy.wait()
    wts_steps[1]()
    keys_values(0)
    adp_steps[3]()
    keys_values(1)
    adp_steps[4]()
    wts_steps[2]()
    adp_steps[5]()
    for slot in range(2):
        t = rows_ref[slot]
        r = t // 2
        dsel[z, slot] = adp[r // 8, (r // 2) % SIDE, r % 2, t % 2][0:16]
    dsel_copies = [send(dsel.at[z], dsel.at[z], to) for to in (zp, zm, zo)]
    wo_step1()
    for copy in dsel_copies:
        copy.wait_recv()
    queries(0)
    attention(0)
    att_send(0)
    wo_step2()
    wts_steps[3]()
    queries(1)
    attention(1)
    att_send(1)
    wts_steps[4]()
    wo_step3()
    att_forward(0)
    wts_steps[5]()
    att_done(0)

    def project_out(slot):
        def body(i, _):
            cols = pl.ds(pl.multiple_of(i * 256, 256), 256)
            mixed = dot(att[slot, 0], wo[0, :, cols])
            for zz in range(1, SIDE):
                mixed += dot(att[slot, zz], wo[zz, :, cols])
            hid[slot, :, cols] = (hid[slot, :, cols].astype(F32) + mixed).astype(BF16)
            return 0

        lax.fori_loop(0, 8, body, 0)

    def gate_up(slot):
        def body(i, _):
            cols = pl.ds(pl.multiple_of(i * 256, 256), 256)
            up_cols = pl.ds(pl.multiple_of(i * 256 + 1024, 256), 256)
            gate = dot(nrm[slot], wts[:, :, :, :, :, cols].reshape(2048, 256))
            up = dot(nrm[slot], wts[:, :, :, :, :, up_cols].reshape(2048, 256))
            act[:, cols] = (gate / (1.0 + jnp.exp(-gate)) * up).astype(BF16)
            return 0

        lax.fori_loop(0, 4, body, 0)

    def down(slot, half):
        def body(i, _):
            xx = half * 2 + i // 2
            yy = (i % 2) * 2
            weight = wts[pl.ds(xx, 1), pl.ds(yy, 2), :, :, :, 2048:3072].reshape(256, 1024)
            cols = pl.ds(pl.multiple_of(half * 1024 + i * 256, 256), 256)
            part[slot, :, cols] = dot_t(act[...], weight).astype(BF16)
            return 0

        lax.fori_loop(0, 4, body, 0)

    halves = (pl.ds(0, 1024), pl.ds(1024, 1024))

    def block(index):
        return pl.ds(pl.multiple_of(index * 128, 128), 128)

    rs = {}

    def rs_start(slot, half):
        far, near = (zm, zp) if half == 0 else (zp, zm)
        near_z = nz if half == 0 else pz
        rs[slot, half] = [
            send(part.at[slot, block(oz), halves[half]], xbuf.at[slot, half], far),
            send(part.at[slot, block(near_z), halves[half]], rbuf.at[slot, half], near),
        ]

    def rs_middle(slot, half):
        far = zm if half == 0 else zp
        far_z = pz if half == 0 else nz
        rs[slot, half][0].wait_recv()
        xbuf[slot, half] = (
            xbuf[slot, half].astype(F32) + part[slot, block(far_z), halves[half]].astype(F32)
        ).astype(BF16)
        rs[slot, half].append(send(xbuf.at[slot, half], ybuf.at[slot, half], far))

    def rs_finish(slot, half):
        rs[slot, half][1].wait_recv()
        rs[slot, half][2].wait_recv()
        total = part[slot, block(z), halves[half]].astype(F32) + rbuf[slot, half].astype(F32)
        total += ybuf[slot, half].astype(F32) + hid[slot, block(z), halves[half]].astype(F32)
        outb[slot, block(z), halves[half]] = total.astype(BF16)

    ag = {}

    def ag_start(slot):
        mine = outb.at[slot, block(z)]
        ag[slot] = [send(mine, mine, zp), send(mine, mine, zm)]

    def ag_forward(slot):
        for copy in ag[slot]:
            copy.wait_recv()
        left, right = outb.at[slot, block(nz), halves[0]], outb.at[slot, block(pz), halves[1]]
        ag[slot] = [send(left, left, zm), send(right, right, zp)]

    def ag_done(slot):
        for copy in ag[slot]:
            copy.wait_recv()
        fetch(outb.at[slot], out_h.at[slot])

    project_out(0)
    att_forward(1)
    normalise(0, gain_mlp)
    gate_up(0)
    for half in range(2):
        down(0, half)
        rs_start(0, half)
    att_done(1)
    project_out(1)
    normalise(1, gain_mlp)
    for half in range(2):
        rs_middle(0, half)
    gate_up(1)
    for half in range(2):
        rs_finish(0, half)
    ag_start(0)
    for half in range(2):
        down(1, half)
        rs_start(1, half)
    ag_forward(0)
    for half in range(2):
        rs_middle(1, half)
    ag_done(0)
    for half in range(2):
        rs_finish(1, half)
    ag_start(1)
    ag_forward(1)
    ag_done(1)
    for copy in sent:
        copy.wait_send()
    for copy in locals_[-2:]:
        copy.wait()


def layer(table_rows, gain_attn, gain_mlp, hidden, wqkv, wout, weights, adapters):
    cosines, sines = rope_tables(512)
    any_space = pl.BlockSpec(memory_space=pl.ANY)
    vmem = pl.BlockSpec(memory_space=pltpu.VMEM)
    copies = 96
    return pl.pallas_call(
        layer_kernel,
        out_shape=jax.ShapeDtypeStruct((2, 512, 2048), BF16),
        in_specs=[pl.BlockSpec(memory_space=pltpu.SMEM)] + [vmem] * 4 + [any_space] * 5,
        out_specs=any_space,
        scratch_shapes=[
            pltpu.VMEM((2, 512, 2048), BF16),
            pltpu.VMEM((3, 2048, 512), BF16),
            pltpu.VMEM((2, 512, 2048), BF16),
            pltpu.VMEM((2, 512, 512), BF16),
            pltpu.VMEM((2, 512, 512), BF16),
            pltpu.VMEM((2, 512, 512), BF16),
            pltpu.VMEM((2, SIDE, 512, 512), BF16),
            pltpu.VMEM((SIDE, 512, 2048), BF16),
            pltpu.VMEM((SIDE, SIDE, 2, 2, 32, 3072), BF16),
            pltpu.VMEM((SIDE, SIDE, 2, 2, 32, 512), BF16),
            pltpu.VMEM((SIDE, 2, 16, 512), BF16),
            pltpu.VMEM((2, 512, 2048), BF16),
            pltpu.VMEM((512, 1024), BF16),
            pltpu.VMEM((2, 512, 2048), BF16),
            pltpu.VMEM((2, 2, 128, 1024), BF16),
            pltpu.VMEM((2, 2, 128, 1024), BF16),
            pltpu.VMEM((2, 2, 128, 1024), BF16),
            pltpu.SemaphoreType.DMA((8,)),
            pltpu.SemaphoreType.DMA((copies,)),
            pltpu.SemaphoreType.DMA((copies,)),
        ],
        compiler_params=pltpu.CompilerParams(
            collective_id=0, has_side_effects=True, vmem_limit_bytes=67_000_000
        ),
        name="layer",
    )(table_rows, gain_attn[None, :], gain_mlp[None, :], jnp.asarray(cosines), jnp.asarray(sines),
      hidden, wqkv, wout, weights, adapters)


def per_device(
    hidden_in, lengths, slot_request, adapter_of, adapter_slot, norm_gain_attn, norm_gain_mlp, final_gain,
    w_qkv, w_out, w_gateup, w_down, adapter_down, adapter_up, vocab,
):
    req_index = lax.axis_index("req")
    mlp_index = lax.axis_index("mlp")
    slots_number, sequence_length, width = hidden_in.shape
    requests = lax.dynamic_slice_in_dim(slot_request, req_index * slots_number, slots_number)
    own_lengths = jnp.take(lengths, requests)
    table_rows = jnp.take(adapter_slot, jnp.take(adapter_of, requests))
    positions = jnp.arange(sequence_length, dtype=jnp.int32)
    weights = jnp.concatenate([w_gateup.reshape(64, 2048), w_down.T], axis=1).reshape(2, 32, 3072)
    down_quarter = lax.dynamic_slice_in_dim(adapter_down, mlp_index * 512, 512, axis=2)
    adapters = jnp.concatenate([down_quarter, adapter_up], axis=1)
    result = layer(
        table_rows, norm_gain_attn, norm_gain_mlp, hidden_in,
        w_qkv.transpose(1, 0, 2), w_out, weights, adapters,
    )
    live = positions[None, :] < own_lengths[:, None]
    out_hidden = jnp.where(live[:, :, None], result, jnp.zeros_like(result))
    out_float = out_hidden.astype(F32)
    square_sum = jnp.sum(out_float * out_float, axis=(1, 2))
    slot_norm = jnp.sqrt(square_sum / (own_lengths.astype(F32) * width))
    last_rows = jnp.stack([
        lax.dynamic_index_in_dim(result[slot], own_lengths[slot] - 1, 0, keepdims=False)
        for slot in range(slots_number)
    ]).astype(F32)
    last_normed = rms_norm(last_rows, final_gain).astype(BF16)
    every_last = lax.all_gather(last_normed, "req", axis=0, tiled=True)
    logits = lax.dot_general(every_last, vocab, (((1,), (1,)), ((), ())), preferred_element_type=F32)
    own_peak = jnp.max(logits, axis=1)
    padded_norm = jnp.zeros_like(own_peak)
    padded_norm = lax.dynamic_update_slice_in_dim(padded_norm, slot_norm, req_index * slots_number, 0)
    everything = lax.all_gather(jnp.stack([own_peak, padded_norm]), ("req", "mlp"), axis=0, tiled=False)
    slot_peak = jnp.max(everything[:, 0], axis=0)
    every_norm = jnp.max(everything[:, 1], axis=0)
    request_total = slot_request.shape[0]
    owners = slot_request[None, :] == jnp.arange(request_total, dtype=jnp.int32)[:, None]
    request_norm = jnp.sum(jnp.where(owners, every_norm[None, :], 0.0), axis=1)
    request_peak = jnp.sum(jnp.where(owners, slot_peak[None, :], 0.0), axis=1)
    return (out_hidden, request_norm, request_peak)


def solution(mesh):
    return jax.shard_map(
        per_device,
        mesh=mesh,
        in_specs=(
            P("req", None, None), P(), P(), P(), P(), P(), P(), P(),
            P(None, None, "mlp"), P("mlp", None), P("req", None, "mlp"), P("mlp", "req"),
            P("req", None, None), P("req", None, "mlp"), P(("req", "mlp"), None),
        ),
        out_specs=(P("req", None, None), P(), P()),
        check_vma=False,
    )
```

```python
import functools

import jax
import jax.numpy as jnp
import numpy as np
from jax import lax
from jax.experimental import pallas as pl
from jax.experimental.pallas import tpu as pltpu
from jax.sharding import PartitionSpec as P

HEAD_WIDTH = 64
EPSILON = 1e-05
ROPE_BASE = 130000.0
ADAPTER_SCALE = 2.0
MASKED = -1e30
MESH = pl.DeviceIdType.MESH
F32 = jnp.float32
BF16 = jnp.bfloat16
SIDE = 4


def rms_norm(values, gain):
    return values * lax.rsqrt(jnp.mean(values * values, axis=-1, keepdims=True) + EPSILON) * gain


def rope_tables(length):
    half = HEAD_WIDTH // 2
    frequency = ROPE_BASE ** (-(np.arange(half, dtype=np.float64) * 2.0 / HEAD_WIDTH))
    angles = np.arange(length, dtype=np.float64)[:, None] * frequency[None, :]
    cosine, sine = np.cos(angles), np.sin(angles)
    cosines = np.concatenate([cosine, cosine] * 2, axis=1).astype(np.float32)
    sines = np.concatenate([-sine, sine] * 2, axis=1).astype(np.float32)
    return cosines, sines


def dot(a, b):
    return jnp.dot(a, b, preferred_element_type=F32)


def dot_t(a, b):
    return lax.dot_general(a, b, (((1,), (1,)), ((), ())), preferred_element_type=F32)


def layer_kernel(
    lengths_ref, request_ref, adapter_ref, row_ref, gain_attn, gain_mlp, gain_last, cos_ref, sin_ref,
    hid_h, wqkv_h, wout_h, wts_h, adp_h, vocab_h,
    out_h, ends_ref,
    hid, wqkv, nrm, qb, kb, vb, att, wo, wts, adp, dsel, part, act, outb, xbuf, rbuf, ybuf,
    vocab, zbuf, lasts, every, peak_zc, peak_x, peak_y,
    local_sem, send_sem, recv_sem,
):
    me = lax.axis_index("req")
    z = lax.axis_index("mlp")
    x, y, c = me // 8, (me // 2) % SIDE, me % 2
    nx, px = lax.rem(x + 1, SIDE), lax.rem(x + 3, SIDE)
    ny, py = lax.rem(y + 1, SIDE), lax.rem(y + 3, SIDE)
    nz, pz, oz = lax.rem(z + 1, SIDE), lax.rem(z + 3, SIDE), lax.rem(z + 2, SIDE)
    ox, oy = lax.rem(x + 2, SIDE), lax.rem(y + 2, SIDE)

    def at(xx, yy):
        return (xx * 8 + yy * 2 + c, z)

    xp, xm, yp, ym = at(nx, y), at(px, y), at(x, ny), at(x, py)
    zp, zm, zo = (me, nz), (me, pz), (me, oz)
    xo, yo = at(ox, y), at(x, oy)
    twin_req = x * 8 + y * 2 + (1 - c)
    twin = (twin_req, z)
    others_zc = [zp, zm, zo, twin, (twin_req, nz), (twin_req, pz), (twin_req, oz)]
    others_x, others_y = [xp, xm, xo], [yp, ym, yo]

    barrier = pltpu.get_barrier_semaphore()
    for other in others_x + others_y + others_zc:
        pl.semaphore_signal(barrier, inc=1, device_id=other, device_id_type=MESH)
    pl.semaphore_wait(barrier, 13)

    lengths, table_rows = [], []
    for slot in range(2):
        request = request_ref[me * 2 + slot]
        lengths.append(lengths_ref[request])
        table_rows.append(row_ref[adapter_ref[request]])

    sent = []

    def send(src, dst, to):
        i = len(sent)
        copy = pltpu.make_async_remote_copy(
            src_ref=src, dst_ref=dst, send_sem=send_sem.at[i], recv_sem=recv_sem.at[i],
            device_id=to, device_id_type=MESH,
        )
        copy.start()
        sent.append(copy)
        return copy

    locals_ = []

    def fetch(src, dst):
        copy = pltpu.make_async_copy(src, dst, local_sem.at[len(locals_)])
        copy.start()
        locals_.append(copy)
        return copy

    def gather_xy(src, full):
        width = src.shape[-1] // 2
        left, right = pl.ds(0, width), pl.ds(width, width)
        state = {}

        def step0():
            state["own"] = fetch(src, full.at[x, y, c])
            own_l, own_r = full.at[x, y, c, :, :, left], full.at[x, y, c, :, :, right]
            state["a"] = [
                send(src.at[:, :, left], own_l, xp), send(src.at[:, :, left], own_l, xm),
                send(src.at[:, :, right], own_r, yp), send(src.at[:, :, right], own_r, ym),
            ]

        def step1():
            for copy in state["a"]:
                copy.wait_recv()
            state["b"] = [
                send(full.at[px, y, c, 0:1, :, left], full.at[px, y, c, 0:1, :, left], xp),
                send(full.at[nx, y, c, 1:2, :, left], full.at[nx, y, c, 1:2, :, left], xm),
                send(full.at[x, py, c, 0:1, :, right], full.at[x, py, c, 0:1, :, right], yp),
                send(full.at[x, ny, c, 1:2, :, right], full.at[x, ny, c, 1:2, :, right], ym),
            ]

        def step2():
            state["own"].wait()
            for copy in state["b"]:
                copy.wait_recv()
            line_l, line_r = full.at[:, y, c, :, :, left], full.at[x, :, c, :, :, right]
            state["c"] = [
                send(line_l, line_l, yp), send(line_l, line_l, ym),
                send(line_r, line_r, xp), send(line_r, line_r, xm),
            ]
            state["t"] = [send(line_l, line_l, twin), send(line_r, line_r, twin)]

        def step3():
            for copy in state["c"]:
                copy.wait_recv()
            state["d"] = [
                send(full.at[0:2, py, c, :, :, left], full.at[0:2, py, c, :, :, left], yp),
                send(full.at[2:4, ny, c, :, :, left], full.at[2:4, ny, c, :, :, left], ym),
                send(full.at[px, 0:2, c, :, :, right], full.at[px, 0:2, c, :, :, right], xp),
                send(full.at[nx, 2:4, c, :, :, right], full.at[nx, 2:4, c, :, :, right], xm),
            ]
            for yy in (py, ny):
                state["t"].append(send(full.at[:, yy, c, :, :, left], full.at[:, yy, c, :, :, left], twin))
            for xx in (px, nx):
                state["t"].append(send(full.at[xx, :, c, :, :, right], full.at[xx, :, c, :, :, right], twin))

        def step4():
            for copy in state["d"]:
                copy.wait_recv()
            state["t"].append(send(full.at[:, oy, c, :, :, left], full.at[:, oy, c, :, :, left], twin))
            state["t"].append(send(full.at[ox, :, c, :, :, right], full.at[ox, :, c, :, :, right], twin))

        def step5():
            for copy in state["t"]:
                copy.wait_recv()

        return [step0, step1, step2, step3, step4, step5]

    adp_steps = gather_xy(adp_h, adp)
    wts_steps = gather_xy(wts_h, wts)
    wo_state = {}

    def wo_step0():
        mine = pl.ds(pl.multiple_of(c * 256, 256), 256)
        wo_state["own"] = fetch(wout_h, wo.at[z])
        wo_state["a"] = [
            send(wout_h.at[mine], wo.at[z, mine], zp), send(wout_h.at[mine], wo.at[z, mine], zm),
        ]

    def wo_step1():
        mine = pl.ds(pl.multiple_of(c * 256, 256), 256)
        low = pl.ds(pl.multiple_of(c * 256, 256), 128)
        high = pl.ds(pl.multiple_of(c * 256 + 128, 128), 128)
        for copy in wo_state["a"]:
            copy.wait_recv()
        wo_state["b"] = [
            send(wo.at[pz, low], wo.at[pz, low], zp), send(wo.at[nz, high], wo.at[nz, high], zm),
        ]
        wo_state["t"] = [
            send(wo.at[pz, mine], wo.at[pz, mine], twin), send(wo.at[nz, mine], wo.at[nz, mine], twin),
        ]

    def wo_step2():
        mine = pl.ds(pl.multiple_of(c * 256, 256), 256)
        for copy in wo_state["b"]:
            copy.wait_recv()
        wo_state["t"].append(send(wo.at[oz, mine], wo.at[oz, mine], twin))

    def wo_step3():
        wo_state["own"].wait()
        for copy in wo_state["t"]:
            copy.wait_recv()

    hid_copy = fetch(hid_h, hid)
    adp_steps[0]()
    wqkv_copy = fetch(wqkv_h, wqkv)
    wts_steps[0]()
    wo_step0()
    vocab_copy = fetch(vocab_h, vocab)

    def normalise(slot, gain):
        def body(i, _):
            rows = pl.ds(pl.multiple_of(i * 32, 32), 32)
            values = hid[slot, rows, :].astype(F32)
            nrm[slot, rows, :] = rms_norm(values, gain[...]).astype(BF16)
            return 0

        lax.fori_loop(0, 16, body, 0)

    lane = lax.broadcasted_iota(jnp.int32, (512, 128), 1)
    first_half = lax.rem(lane, 64) < 32

    def rotate(values):
        swapped = jnp.where(first_half, pltpu.roll(values, 96, 1), pltpu.roll(values, 32, 1))
        return values * cos_ref[...] + swapped * sin_ref[...]

    def keys_values(slot):
        def body(i, _):
            cols = pl.ds(pl.multiple_of(i * 256, 256), 256)
            keys = dot(nrm[slot], wqkv[1, :, cols])
            kb[slot, :, pl.ds(pl.multiple_of(i * 256, 256), 128)] = rotate(keys[:, :128]).astype(BF16)
            kb[slot, :, pl.ds(pl.multiple_of(i * 256 + 128, 128), 128)] = rotate(keys[:, 128:]).astype(BF16)
            vb[slot, :, cols] = dot(nrm[slot], wqkv[2, :, cols]).astype(BF16)
            return 0

        lax.fori_loop(0, 2, body, 0)

    def queries(slot):
        low = dot_t(nrm[slot, :, 0:512], dsel[0, slot])
        for zz in range(1, SIDE):
            low += dot_t(nrm[slot, :, zz * 512:(zz + 1) * 512], dsel[zz, slot])
        low = low.astype(BF16)
        t = table_rows[slot]
        r = t // 2

        def body(i, _):
            cols = pl.ds(pl.multiple_of(i * 256, 256), 256)
            up = adp[r // 8, (r // 2) % SIDE, r % 2, t % 2][16:32]
            up_low, up_high = up[:, :256], up[:, 256:]
            up_cols = jnp.where(i == 0, up_low, up_high)
            values = dot(nrm[slot], wqkv[0, :, cols]) + ADAPTER_SCALE * dot(low, up_cols)
            scale = HEAD_WIDTH ** (-0.5)
            qb[slot, :, pl.ds(pl.multiple_of(i * 256, 256), 128)] = (rotate(values[:, :128]) * scale).astype(BF16)
            qb[slot, :, pl.ds(pl.multiple_of(i * 256 + 128, 128), 128)] = (rotate(values[:, 128:]) * scale).astype(BF16)
            return 0

        lax.fori_loop(0, 2, body, 0)

    lane_q = lax.broadcasted_iota(jnp.int32, (128, 128), 1) < 64
    causal = lax.broadcasted_iota(jnp.int32, (128, 128), 1) <= lax.broadcasted_iota(jnp.int32, (128, 128), 0)
    causal2 = jnp.concatenate([causal, causal], axis=0)

    def attention(slot):
        def body(i, _):
            cols = pl.ds(pl.multiple_of(i * 128, 128), 128)
            for j in range(4):
                q = qb[slot, j * 128:(j + 1) * 128, cols]
                zero = jnp.zeros_like(q)
                both = jnp.concatenate([jnp.where(lane_q, q, zero), jnp.where(lane_q, zero, q)], axis=0)
                n = (j + 1) * 128
                scores = dot_t(both, kb[slot, 0:n, cols])
                diag = jnp.where(causal2, scores[:, n - 128:], MASKED)
                scores = diag if j == 0 else jnp.concatenate([scores[:, :n - 128], diag], axis=1)
                top = jnp.max(scores, axis=1, keepdims=True)
                weights = jnp.exp(scores - top)
                total = jnp.sum(weights, axis=1, keepdims=True)
                mixed = dot(weights.astype(BF16), vb[slot, 0:n, cols]) / total
                att[slot, z, j * 128:(j + 1) * 128, cols] = jnp.where(lane_q, mixed[:128], mixed[128:]).astype(BF16)
            return 0

        lax.fori_loop(0, 4, body, 0)

    att_state = {}

    def att_send(slot):
        mine = att.at[slot, z]
        att_state[slot] = [send(mine, mine, zp), send(mine, mine, zm)]

    def att_forward(slot):
        for copy in att_state[slot]:
            copy.wait_recv()
        low, high = att.at[slot, pz, 0:256], att.at[slot, nz, 256:512]
        att_state[slot] = [send(low, low, zp), send(high, high, zm)]

    def att_done(slot):
        for copy in att_state[slot]:
            copy.wait_recv()

    hid_copy.wait()
    normalise(0, gain_attn)
    adp_steps[1]()
    normalise(1, gain_attn)
    adp_steps[2]()
    wqkv_copy.wait()
    wts_steps[1]()
    keys_values(0)
    adp_steps[3]()
    keys_values(1)
    adp_steps[4]()
    wts_steps[2]()
    adp_steps[5]()
    for slot in range(2):
        t = table_rows[slot]
        r = t // 2
        dsel[z, slot] = adp[r // 8, (r // 2) % SIDE, r % 2, t % 2][0:16]
    dsel_copies = [send(dsel.at[z], dsel.at[z], to) for to in (zp, zm, zo)]
    wo_step1()
    for copy in dsel_copies:
        copy.wait_recv()
    queries(0)
    attention(0)
    att_send(0)
    wo_step2()
    wts_steps[3]()
    queries(1)
    attention(1)
    att_send(1)
    wts_steps[4]()
    wo_step3()
    att_forward(0)
    wts_steps[5]()
    att_done(0)

    def project_out(slot):
        def body(i, _):
            cols = pl.ds(pl.multiple_of(i * 256, 256), 256)
            mixed = dot(att[slot, 0], wo[0, :, cols])
            for zz in range(1, SIDE):
                mixed += dot(att[slot, zz], wo[zz, :, cols])
            hid[slot, :, cols] = (hid[slot, :, cols].astype(F32) + mixed).astype(BF16)
            return 0

        lax.fori_loop(0, 8, body, 0)

    def gate_up(slot):
        def body(i, _):
            cols = pl.ds(pl.multiple_of(i * 256, 256), 256)
            up_cols = pl.ds(pl.multiple_of(i * 256 + 1024, 256), 256)
            gate = dot(nrm[slot], wts[:, :, :, :, :, cols].reshape(2048, 256))
            up = dot(nrm[slot], wts[:, :, :, :, :, up_cols].reshape(2048, 256))
            act[:, cols] = (gate / (1.0 + jnp.exp(-gate)) * up).astype(BF16)
            return 0

        lax.fori_loop(0, 4, body, 0)

    def down(slot, half):
        def body(i, _):
            xx = half * 2 + i // 2
            yy = (i % 2) * 2
            weight = wts[pl.ds(xx, 1), pl.ds(yy, 2), :, :, :, 2048:3072].reshape(256, 1024)
            cols = pl.ds(pl.multiple_of(half * 1024 + i * 256, 256), 256)
            part[slot, :, cols] = dot_t(act[...], weight).astype(BF16)
            return 0

        lax.fori_loop(0, 4, body, 0)

    halves = (pl.ds(0, 1024), pl.ds(1024, 1024))

    def block(index):
        return pl.ds(pl.multiple_of(index * 128, 128), 128)

    rs = {}

    def rs_start(slot, half):
        far, near = (zm, zp) if half == 0 else (zp, zm)
        near_z = nz if half == 0 else pz
        rs[slot, half] = [
            send(part.at[slot, block(oz), halves[half]], xbuf.at[slot, half], far),
            send(part.at[slot, block(near_z), halves[half]], rbuf.at[slot, half], near),
        ]

    def rs_middle(slot, half):
        far = zm if half == 0 else zp
        far_z = pz if half == 0 else nz
        rs[slot, half][0].wait_recv()
        xbuf[slot, half] = (
            xbuf[slot, half].astype(F32) + part[slot, block(far_z), halves[half]].astype(F32)
        ).astype(BF16)
        rs[slot, half].append(send(xbuf.at[slot, half], ybuf.at[slot, half], far))

    def rs_finish(slot, half):
        rs[slot, half][1].wait_recv()
        rs[slot, half][2].wait_recv()
        total = part[slot, block(z), halves[half]].astype(F32) + rbuf[slot, half].astype(F32)
        total += ybuf[slot, half].astype(F32) + hid[slot, block(z), halves[half]].astype(F32)
        position = lax.broadcasted_iota(jnp.int32, total.shape, 0) + z * 128
        live = jnp.where(position < lengths[slot], total, 0.0).astype(BF16)
        outb[slot, block(z), halves[half]] = live
        live = live.astype(F32)
        last = jnp.where(position == lengths[slot] - 1, live, 0.0)
        zbuf[z, slot:slot + 1, halves[half]] = jnp.sum(last, axis=0, keepdims=True)
        zbuf[z, slot + 2:slot + 3, halves[half]] = jnp.sum(live * live, axis=0, keepdims=True)

    ag = {}

    def ag_start(slot):
        mine = outb.at[slot, block(z)]
        ag[slot] = [send(mine, mine, zp), send(mine, mine, zm)]

    def ag_forward(slot):
        for copy in ag[slot]:
            copy.wait_recv()
        left, right = outb.at[slot, block(nz), halves[0]], outb.at[slot, block(pz), halves[1]]
        ag[slot] = [send(left, left, zm), send(right, right, zp)]

    def ag_done(slot):
        for copy in ag[slot]:
            copy.wait_recv()
        fetch(outb.at[slot], out_h.at[slot])

    project_out(0)
    att_forward(1)
    normalise(0, gain_mlp)
    gate_up(0)
    for half in range(2):
        down(0, half)
        rs_start(0, half)
    att_done(1)
    project_out(1)
    normalise(1, gain_mlp)
    for half in range(2):
        rs_middle(0, half)
    gate_up(1)
    for half in range(2):
        rs_finish(0, half)
    ag_start(0)
    for half in range(2):
        down(1, half)
        rs_start(1, half)
    ag_forward(0)
    for half in range(2):
        rs_middle(1, half)
    ag_done(0)
    for half in range(2):
        rs_finish(1, half)
    last_copies = [send(zbuf.at[z], zbuf.at[z], to) for to in (zp, zm, zo)]
    ag_start(1)
    for copy in last_copies:
        copy.wait_recv()
    rows = (zbuf[0] + zbuf[1]) + (zbuf[2] + zbuf[3])
    squares = jnp.sum(rows, axis=1, keepdims=True)
    lasts[x, y, c] = rms_norm(rows[0:2], gain_last[...]).astype(BF16)
    mine = lasts.at[x, y, c]
    line_copies = [send(mine, mine, to) for to in others_x]
    for copy in line_copies:
        copy.wait_recv()
    line = lasts.at[:, y, c]
    plane_copies = [send(line, line, to) for to in others_y]
    twin_copies = [send(line, line, twin)]
    ag_forward(1)
    for copy in plane_copies:
        copy.wait_recv()
    for yy in (ny, py, oy):
        line = lasts.at[:, yy, c]
        twin_copies.append(send(line, line, twin))
    vocab_copy.wait()
    for copy in twin_copies:
        copy.wait_recv()
    for r in range(32):
        every[2 * r:2 * r + 2, :] = lasts[r // 8, (r // 2) % SIDE, r % 2].astype(F32)
    logits = dot_t(vocab[...], every[...].astype(BF16))
    lane_r = lax.broadcasted_iota(jnp.int32, (1, 64), 1)
    norms = jnp.zeros((1, 64), F32)
    for slot in range(2):
        mean = squares[slot + 2:slot + 3] / (lengths[slot].astype(F32) * 2048.0)
        norms = jnp.where(lane_r == me * 2 + slot, jnp.sqrt(mean), norms)
    row_r = lax.broadcasted_iota(jnp.int32, (8, 64), 0)
    peak_zc[z, c] = jnp.where(row_r == 0, jnp.max(logits, axis=0, keepdims=True), norms)
    peak_copies = [send(peak_zc.at[z, c], peak_zc.at[z, c], to) for to in others_zc]
    ag_done(1)
    for copy in peak_copies:
        copy.wait_recv()
    peak_x[x] = jnp.max(peak_zc[...].reshape(8, 8, 64), axis=0)
    peak_copies = [send(peak_x.at[x], peak_x.at[x], to) for to in others_x]
    for copy in peak_copies:
        copy.wait_recv()
    peak_y[y] = jnp.max(peak_x[...], axis=0)
    peak_copies = [send(peak_y.at[y], peak_y.at[y], to) for to in others_y]
    for copy in peak_copies:
        copy.wait_recv()
    ends_ref[...] = jnp.max(peak_y[...], axis=0)
    for copy in sent:
        copy.wait_send()
    for copy in locals_[-2:]:
        copy.wait()


def layer(tables, gains, hidden, wqkv, wout, weights, adapters, vocab):
    cosines, sines = rope_tables(512)
    any_space = pl.BlockSpec(memory_space=pl.ANY)
    vmem = pl.BlockSpec(memory_space=pltpu.VMEM)
    copies = 136
    return pl.pallas_call(
        layer_kernel,
        out_shape=(jax.ShapeDtypeStruct((2, 512, 2048), BF16), jax.ShapeDtypeStruct((8, 64), F32)),
        in_specs=[pl.BlockSpec(memory_space=pltpu.SMEM)] * 4 + [vmem] * 5 + [any_space] * 6,
        out_specs=(any_space, vmem),
        scratch_shapes=[
            pltpu.VMEM((2, 512, 2048), BF16),
            pltpu.VMEM((3, 2048, 512), BF16),
            pltpu.VMEM((2, 512, 2048), BF16),
            pltpu.VMEM((2, 512, 512), BF16),
            pltpu.VMEM((2, 512, 512), BF16),
            pltpu.VMEM((2, 512, 512), BF16),
            pltpu.VMEM((2, SIDE, 512, 512), BF16),
            pltpu.VMEM((SIDE, 512, 2048), BF16),
            pltpu.VMEM((SIDE, SIDE, 2, 2, 32, 3072), BF16),
            pltpu.VMEM((SIDE, SIDE, 2, 2, 32, 512), BF16),
            pltpu.VMEM((SIDE, 2, 16, 512), BF16),
            pltpu.VMEM((2, 512, 2048), BF16),
            pltpu.VMEM((512, 1024), BF16),
            pltpu.VMEM((2, 512, 2048), BF16),
            pltpu.VMEM((2, 2, 128, 1024), BF16),
            pltpu.VMEM((2, 2, 128, 1024), BF16),
            pltpu.VMEM((2, 2, 128, 1024), BF16),
            pltpu.VMEM((384, 2048), BF16),
            pltpu.VMEM((SIDE, 4, 2048), F32),
            pltpu.VMEM((SIDE, SIDE, 2, 2, 2048), BF16),
            pltpu.VMEM((64, 2048), F32),
            pltpu.VMEM((SIDE, 2, 8, 64), F32),
            pltpu.VMEM((SIDE, 8, 64), F32),
            pltpu.VMEM((SIDE, 8, 64), F32),
            pltpu.SemaphoreType.DMA((8,)),
            pltpu.SemaphoreType.DMA((copies,)),
            pltpu.SemaphoreType.DMA((copies,)),
        ],
        compiler_params=pltpu.CompilerParams(
            collective_id=0, has_side_effects=True, vmem_limit_bytes=67_000_000
        ),
        name="layer",
    )(*tables, *(gain[None, :] for gain in gains), jnp.asarray(cosines), jnp.asarray(sines),
      hidden, wqkv, wout, weights, adapters, vocab)


def per_device(
    hidden_in, lengths, slot_request, adapter_of, adapter_slot, norm_gain_attn, norm_gain_mlp, final_gain,
    w_qkv, w_out, w_gateup, w_down, adapter_down, adapter_up, vocab,
):
    mlp_index = lax.axis_index("mlp")
    weights = jnp.concatenate([w_gateup.reshape(64, 2048), w_down.T], axis=1).reshape(2, 32, 3072)
    down_quarter = lax.dynamic_slice_in_dim(adapter_down, mlp_index * 512, 512, axis=2)
    adapters = jnp.concatenate([down_quarter, adapter_up], axis=1)
    out_hidden, ends = layer(
        (lengths, slot_request, adapter_of, adapter_slot), (norm_gain_attn, norm_gain_mlp, final_gain),
        hidden_in, w_qkv.transpose(1, 0, 2), w_out, weights, adapters, vocab,
    )
    owners = slot_request[None, :] == jnp.arange(slot_request.shape[0], dtype=jnp.int32)[:, None]
    by_request = jnp.sum(jnp.where(owners[None], ends[0:2, None, :], 0.0), axis=2)
    return (out_hidden, by_request[1], by_request[0])


def solution(mesh):
    return jax.shard_map(
        per_device,
        mesh=mesh,
        in_specs=(
            P("req", None, None), P(), P(), P(), P(), P(), P(), P(),
            P(None, None, "mlp"), P("mlp", None), P("req", None, "mlp"), P("mlp", "req"),
            P("req", None, None), P("req", None, "mlp"), P(("req", "mlp"), None),
        ),
        out_specs=(P("req", None, None), P(), P()),
        check_vma=False,
    )
```
